32 devices in a mesh: term: 2 (over x), sector: 16 (over z, y, core).
Axes of the slice: x: 2, y: 2, z: 4, core: 2. Of those that a mesh axis runs over, the one named last changes fastest.
Arguments:
- psi_start: bfloat16 [128, 256, 256], P('sector'), may hold values from -6 to 6
- left_env: bfloat16 [6, 128, 256, 256], P('term', 'sector')
- right_env: bfloat16 [6, 128, 256, 256], P('term', 'sector')
- connect: int32 [6, 128], P('term', 'sector'), may hold values from 0 to 127, as said below
- sector_dims: int32 [2, 128], P(None, 'sector'), may hold values from 64 to 256
- precond: bfloat16 [128, 256, 256], P('sector'), may hold values from 0.5 to 4
Outputs:
- projected: float32 [3, 3], replicated
- last_vector: float32 [128, 256, 256], P('sector', 'term')
- new_env: bfloat16 [6, 128, 256, 256], P('term', 'sector')
The draws below stay inside these ranges and needn't reach their ends.
Inputs may be any that keep to these rules, and one draw needn't show every extreme that they name: connect[t, s] differs from s by at most 8.
All inputs are finite; a program needn't handle non-finite values.
Results may differ from the reference program's by a relative error of at most 0.012.
Values may be sent and summed in bfloat16 or wider, within the bound.
A program may use at most 128 MiB of HBM per device.

```python
import math
import jax
import jax.numpy as jnp
from jax import lax

DB = 256
SD = 8
TD = 3
SECTORS = 128
TERMS = 6


identity_weight = 0.06


drawn_spread = 0.5


shifted_spread = 0.3


def shift_terms():
    return jnp.arange(TERMS) % TD == TD - 1


def unit_diagonal():
    row_ids = lax.broadcasted_iota(jnp.int32, (DB, DB), 0)
    col_ids = lax.broadcasted_iota(jnp.int32, (DB, DB), 1)
    return (row_ids == col_ids).astype(jnp.float32)


def draw_left_env(key, part):
    noise_key, device_key, sector_key = jax.random.split(jax.random.fold_in(key, 17), 3)
    full_shape = (TERMS, SECTORS, DB, DB)
    noise = jax.random.normal(noise_key, full_shape, jnp.float32)
    scaled = noise * DB ** (-0.5)
    device_scale = jnp.exp(jax.random.uniform(device_key, (SECTORS // SD,), jnp.float32, math.log(0.1), math.log(1.0)))
    sector_scale = jnp.exp(jax.random.uniform(sector_key, (SECTORS,), jnp.float32, math.log(0.6), math.log(1.6)))
    energies = jnp.repeat(device_scale, SD) * sector_scale
    shifted = identity_weight * (energies[None, :, None, None] * unit_diagonal()[None, None] + shifted_spread * scaled)
    drawn = drawn_spread * scaled
    return jnp.where(shift_terms()[:, None, None, None], shifted, drawn).astype(jnp.bfloat16)


def draw_right_env(key, part):
    noise_key = jax.random.fold_in(key, 29)
    full_shape = (TERMS, SECTORS, DB, DB)
    noise = jax.random.normal(noise_key, full_shape, jnp.float32)
    scaled = noise * DB ** (-0.5)
    shift_count = TERMS // TD
    right_scale = 2.0 / (shift_count * identity_weight)
    shifted = right_scale * (unit_diagonal()[None, None] + shifted_spread * scaled)
    drawn = drawn_spread * scaled
    return jnp.where(shift_terms()[:, None, None, None], shifted, drawn).astype(jnp.bfloat16)


def draw_connect(key, part):
    offsets = jax.random.randint(jax.random.fold_in(key, 5), (TERMS, SECTORS), -SD, SD + 1)
    places = jnp.arange(SECTORS)[None, :]
    term_ids = jnp.arange(TERMS)[:, None]
    lower = (places % SD == 0) & (term_ids == 0)
    upper = (places % SD == SD - 1) & (term_ids == 1)
    offsets = jnp.where(lower, -SD, jnp.where(upper, SD, offsets))
    offsets = jnp.where(term_ids % TD == TD - 1, 0, offsets)
    return jnp.clip(places + offsets, 0, SECTORS - 1).astype(jnp.int32)


def plant(array, key, low, top_value):
    longest = array.shape.index(max(array.shape))
    spots = []
    for shift in (0, 1):
        where = [jax.random.randint(jax.random.fold_in(key, axis), (), 0, length) for axis, length in enumerate(array.shape)]
        where[longest] = (where[longest] + shift) % array.shape[longest]
        spots.append(tuple(where))
    return array.at[spots[0]].set(low).at[spots[1]].set(top_value)


def steps_of(key, dims, cuts, low, top_value):
    def one(dim, blocks):
        heights = jax.random.uniform(jax.random.fold_in(jax.random.fold_in(key, 6), dim), (blocks,), jnp.float32, low / len(cuts), top_value / len(cuts))
        return jnp.repeat(jnp.exp(heights), dims[dim] // blocks).reshape((-1,) + (1,) * (len(dims) - dim - 1))

    factor_of = one(*cuts[0])
    for cut in cuts[1:]:
        factor_of = factor_of * one(*cut)
    return factor_of


def gaussian(own_key, dims, spread, reach, cuts=(), dtype=jnp.bfloat16):
    factor_of = steps_of(own_key, dims, cuts, -0.22, 0.18) if cuts else 1.0
    array = jax.random.normal(own_key, dims, jnp.float32) * spread * factor_of
    return jnp.minimum(jnp.maximum(array, -reach), reach).astype(dtype)


def setup_inputs(seed: int = 0) -> dict:
    arg_keys = jax.random.split(jax.random.key(seed), 7)
    psi_start = gaussian(arg_keys[0], (SECTORS, DB, DB), 1.0, 6.0, ((0, 16),))
    left_env = draw_left_env(jax.random.fold_in(arg_keys[6], 71), 0)
    right_env = draw_right_env(jax.random.fold_in(arg_keys[6], 71), 0)
    connect = draw_connect(jax.random.fold_in(arg_keys[6], 71), 0)
    sector_dims = plant(jax.random.randint(arg_keys[4], (2, SECTORS), DB // 4, DB + 1), jax.random.fold_in(arg_keys[4], 1), DB // 4, DB).astype(jnp.int32)
    precond = jnp.clip(jnp.exp(math.log(4.0) - 2.0794415 * jax.random.uniform(arg_keys[5], (SECTORS, DB, DB), jnp.float32) ** steps_of(arg_keys[5], (SECTORS, DB, DB), ((0, 16),), -0.2, 0.2)), 0.5, 4.0).astype(jnp.bfloat16)
    return dict(psi_start=psi_start, left_env=left_env, right_env=right_env, connect=connect, sector_dims=sector_dims, precond=precond)


epsilon = 1e-06

def block_mask(sector_dims):
    row_ids = lax.broadcasted_iota(jnp.int32, (SECTORS, DB, DB), 1)
    col_ids = lax.broadcasted_iota(jnp.int32, (SECTORS, DB, DB), 2)
    keep = (row_ids < sector_dims[0][:, None, None]) & (col_ids < sector_dims[1][:, None, None])
    return keep.astype(jnp.float32)

def apply_terms(vector_b, left_env, right_env, connect, with_env):

    def one_term(total, pieces):
        left_one, right_one, source_one = pieces
        source = vector_b[source_one]
        half = jnp.einsum('sij,sjk->sik', left_one.astype(jnp.float32), source.astype(jnp.float32)).astype(jnp.bfloat16)
        total = total + jnp.einsum('sik,slk->sil', half.astype(jnp.float32), right_one.astype(jnp.float32))
        if with_env:
            env_one = jnp.einsum('sji,sjk->sik', vector_b.astype(jnp.float32), half.astype(jnp.float32)) * DB ** (-0.5)
            return (total, env_one.astype(jnp.bfloat16))
        return (total, None)
    return lax.scan(one_term, jnp.zeros((SECTORS, DB, DB), jnp.float32), (left_env, right_env, connect))

def reference(psi_start, left_env, right_env, connect, sector_dims, precond):
    mask = block_mask(sector_dims)
    entries = float(SECTORS * DB * DB)

    def inner(first, second):
        return jnp.sum(first * second) / entries
    vector = mask * psi_start.astype(jnp.float32)
    vector = vector / jnp.sqrt(inner(vector, vector) + epsilon)
    basis = [vector]
    sigmas = []
    new_env = None
    for which in range(3):
        vector_b = basis[which].astype(jnp.bfloat16)
        if which < 2:
            total, unused = apply_terms(vector_b, left_env, right_env, connect, False)
        else:
            total, new_env = apply_terms(vector_b, left_env, right_env, connect, True)
        sigma = total * mask
        sigmas.append(sigma)
        if which < 2:
            theta = inner(basis[which], sigma)
            corr = (sigma - theta * basis[which]) / precond.astype(jnp.float32)
            correlations = [inner(member, corr) for member in basis]
            for member, weight in zip(basis, correlations):
                corr = corr - weight * member
            corr = corr / jnp.sqrt(inner(corr, corr) + epsilon)
            basis.append(corr)
    projected = jnp.stack([jnp.stack([inner(basis[row], sigmas[col]) for col in range(3)]) for row in range(3)])
    return (projected, basis[2], new_env)
```

```python
import functools
import jax
import jax.numpy as jnp
from jax import lax
from jax.experimental import pallas as pl
from jax.experimental.pallas import tpu as pltpu
from jax.sharding import PartitionSpec as P

epsilon = 1e-06
MESH = pl.DeviceIdType.MESH
F32 = jnp.float32
BF16 = jnp.bfloat16
ROWS = 16


def fold(values):
    rows, width = values.shape
    total = values.reshape(rows // 8, 8, width).sum(axis=0)
    out = total[:, :128]
    for start in range(128, width, 128):
        out = out + total[:, start : start + 128]
    return out


def kernel(
    sizes,
    dims, conn, psi, left, right, pre,
    proj, last, env,
    raw, ext1, ext2, ext3, acc, stage, came, sig1, sig2, base1, base2, tile, slots,
    halo_send, halo_recv, share_send, share_recv, part_send, part_recv, sum_send, sum_recv,
):
    pieces, devices, terms, blocks, width, entries = sizes
    share = width // pieces
    count = pieces * devices
    step = min(32, share)
    steps = share // step
    me_t = lax.axis_index("term")
    me_s = lax.axis_index("sector")
    me = me_t * devices + me_s
    first = me_s * blocks - blocks
    has_low = me_s > 0
    has_high = me_s < devices - 1
    zero = jnp.zeros((8, 128), F32)

    def device_at(offset):
        other = lax.rem(me + offset, count)
        return (other // devices, lax.rem(other, devices))

    def term_at(offset):
        return lax.rem(me_t + offset, pieces)

    def rows_of(piece):
        return pl.ds(pl.multiple_of(piece * share, share), share)

    barrier = pltpu.get_barrier_semaphore()

    @pl.loop(1, count)
    def _(offset):
        pl.semaphore_signal(barrier, inc=1, device_id=device_at(offset), device_id_type=MESH)

    pl.semaphore_wait(barrier, count - 1)

    def halo_copy(ref, s, j, up, rows):
        slot = s if up else 2 * blocks + s
        direction = 0 if up else 1
        return pltpu.make_async_remote_copy(
            src_ref=ref.at[blocks + s, rows],
            dst_ref=ref.at[slot, rows],
            send_sem=halo_send.at[direction, j, s],
            recv_sem=halo_recv.at[direction, j, s],
            device_id=(me_t, me_s + 1 if up else me_s - 1),
            device_id_type=MESH,
        )

    def halo_start(ref, s, j, rows):
        @pl.when(has_high)
        def _():
            halo_copy(ref, s, j, True, rows).start()

        @pl.when(has_low)
        def _():
            halo_copy(ref, s, j, False, rows).start()

    def halo_wait(ref, s, j, rows):
        @pl.when(has_high)
        def _():
            halo_copy(ref, s, j, True, rows).wait_send()
            halo_copy(ref, s, j, False, rows).wait_recv()

        @pl.when(has_low)
        def _():
            halo_copy(ref, s, j, False, rows).wait_send()
            halo_copy(ref, s, j, True, rows).wait_recv()

    def share_copy(ref, s, offset, piece):
        return pltpu.make_async_remote_copy(
            src_ref=ref.at[blocks + s, rows_of(piece)],
            dst_ref=ref.at[blocks + s, rows_of(piece)],
            send_sem=share_send.at[offset - 1, s],
            recv_sem=share_recv.at[offset - 1, s],
            device_id=(term_at(offset), me_s),
            device_id_type=MESH,
        )

    def part_copy(s, offset):
        return pltpu.make_async_remote_copy(
            src_ref=stage.at[offset - 1, s],
            dst_ref=came.at[offset - 1, s],
            send_sem=part_send.at[offset - 1, s],
            recv_sem=part_recv.at[offset - 1, s],
            device_id=(term_at(offset), me_s),
            device_id_type=MESH,
        )

    def sum_start(which, tiles):
        rows = [jnp.sum(one, axis=0, keepdims=True) for one in tiles]
        rows = rows + [jnp.zeros((1, 128), F32)] * (ROWS - len(rows))
        packed = jnp.concatenate(rows, axis=0)
        tile[which] = packed
        slots[which, me] = packed

        @pl.loop(1, count)
        def _(offset):
            pltpu.make_async_remote_copy(
                src_ref=tile.at[which],
                dst_ref=slots.at[which, me],
                send_sem=sum_send.at[which],
                recv_sem=sum_recv.at[which],
                device_id=device_at(offset),
                device_id_type=MESH,
            ).start()

    def sum_finish(which):
        others = slots.at[which, pl.ds(0, count - 1)]
        pltpu.make_async_copy(others, others, sum_recv.at[which]).wait()
        pltpu.make_async_copy(others, others, sum_send.at[which]).wait()
        total = lax.fori_loop(
            0, count, lambda i, t: t + slots[which, i], jnp.zeros((ROWS, 128), F32)
        )
        full = jnp.sum(total, axis=1, keepdims=True) / entries
        return lambda row: full[row : row + 1, :]

    row_ids = lax.broadcasted_iota(jnp.int32, (width, width), 0)
    col_ids = lax.broadcasted_iota(jnp.int32, (width, width), 1)
    all_rows = pl.ds(0, width)

    @pl.loop(0, blocks)
    def _(s):
        keep = (row_ids < dims[0, s]) & (col_ids < dims[1, s])
        raw[blocks + s] = jnp.where(keep, psi[s].astype(F32), 0.0).astype(BF16)
        halo_start(raw, s, 0, all_rows)

    def chunk(i):
        return i // steps, pl.multiple_of(lax.rem(i, steps) * step, step)

    def own_rows(start):
        return pl.ds(pl.multiple_of(me_t * share + start, step), step)

    def norm_step(i, total):
        s, start = chunk(i)
        v = raw[blocks + s, own_rows(start), :].astype(F32)
        return total + fold(v * v)

    sum_start(0, [lax.fori_loop(0, blocks * steps, norm_step, zero)])
    norm = sum_finish(0)(0)
    scale = 1.0 / jnp.sqrt(norm + epsilon)

    def scaled(slot):
        ext1[slot] = (raw[slot].astype(F32) * scale).astype(BF16)

    @pl.loop(0, blocks)
    def _(s):
        scaled(blocks + s)
        base1[s] = raw[blocks + s, rows_of(me_t), :].astype(F32) * scale

    @pl.loop(0, blocks)
    def _(s):
        halo_wait(raw, s, 0, all_rows)

        @pl.when(has_low)
        def _():
            scaled(s)

        @pl.when(has_high)
        def _():
            scaled(2 * blocks + s)

    def product(ref, s, with_env):
        halves = []
        for t in range(terms):
            source = ref[jnp.clip(conn[t, s] - first, 0, 3 * blocks - 1)]
            half = jnp.dot(left[t, s], source, preferred_element_type=F32).astype(BF16)
            halves.append(half)
        total = None
        for t in range(terms):
            one = lax.dot_general(
                halves[t], right[t, s], (((1,), (1,)), ((), ())), preferred_element_type=F32
            )
            total = one if total is None else total + one
            if with_env:
                new = lax.dot_general(
                    ref[blocks + s], halves[t], (((0,), (0,)), ((), ())),
                    preferred_element_type=F32,
                )
                env[t, s] = (new * width ** (-0.5)).astype(BF16)
        return total

    def apply(ref):
        @pl.loop(0, blocks)
        def _(s):
            acc[s] = product(ref, s, False)
            for offset in range(1, pieces):
                stage[offset - 1, s] = acc[s, rows_of(term_at(offset)), :].astype(BF16)
                part_copy(s, offset).start()

    def masked_sum(s, start):
        total = acc[s, own_rows(start), :]
        for offset in range(1, pieces):
            total = total + came[offset - 1, s, pl.ds(start, step), :].astype(F32)
        rows = lax.broadcasted_iota(jnp.int32, (step, width), 0) + (me_t * share + start)
        cols = lax.broadcasted_iota(jnp.int32, (step, width), 1)
        return jnp.where((rows < dims[0, s]) & (cols < dims[1, s]), total, 0.0)

    def divided(s, start):
        return 1.0 / pre[s, own_rows(start), :].astype(F32)

    def part_wait(s):
        for offset in range(1, pieces):
            part_copy(s, offset).wait()

    def spread(ref, out, corr_of, meanwhile=None):
        @pl.loop(0, blocks)
        def _(s):
            @pl.loop(0, steps)
            def _(k):
                start = pl.multiple_of(k * step, step)
                value = corr_of(s, start)
                out[s, pl.ds(start, step), :] = value
                ref[blocks + s, own_rows(start), :] = value.astype(BF16)

            for offset in range(1, pieces):
                share_copy(ref, s, offset, me_t).start()
            halo_start(ref, s, 0, rows_of(me_t))

        @pl.loop(0, blocks)
        def _(s):
            for offset in range(1, pieces):
                share_copy(ref, s, offset, term_at(pieces - offset)).wait_recv()
                halo_start(ref, s, offset, rows_of(term_at(pieces - offset)))

        extra = meanwhile() if meanwhile is not None else None

        @pl.loop(0, blocks)
        def _(s):
            for offset in range(1, pieces):
                share_copy(ref, s, offset, me_t).wait_send()
            for j in range(pieces):
                halo_wait(ref, s, j, rows_of(term_at(pieces - j)))
        return extra

    apply(ext1)

    def sums1(i, totals):
        s, start = chunk(i)
        here = pl.ds(start, step)

        @pl.when(start == 0)
        def _():
            part_wait(s)

        sigma = masked_sum(s, start)
        sig1[s, here, :] = sigma
        inverse = divided(s, start)
        b1 = base1[s, here, :]
        r = sigma * inverse
        q = b1 * inverse
        pairs = [(b1, sigma), (b1, r), (b1, q), (r, r), (r, q), (q, q), (b1, b1)]
        return tuple(t + fold(x * y) for t, (x, y) in zip(totals, pairs))

    sum_start(1, lax.fori_loop(0, blocks * steps, sums1, (zero,) * 7))
    got = sum_finish(1)
    theta1 = got(0)
    first_gram = got(6)
    weight = got(1) - theta1 * got(2)
    length = (
        (got(3) - 2.0 * theta1 * got(4) + theta1 * theta1 * got(5))
        - 2.0 * weight * weight
        + weight * weight * first_gram
    )
    scale1 = 1.0 / jnp.sqrt(jnp.maximum(length, 0.0) + epsilon)

    def corr1(s, start):
        here = pl.ds(start, step)
        b1 = base1[s, here, :]
        corr = (sig1[s, here, :] - theta1 * b1) * divided(s, start)
        return (corr - weight * b1) * scale1

    spread(ext2, base2, corr1)

    apply(ext2)

    def sums2(i, totals):
        s, start = chunk(i)
        here = pl.ds(start, step)

        @pl.when(start == 0)
        def _():
            part_wait(s)

        sigma = masked_sum(s, start)
        sig2[s, here, :] = sigma
        inverse = divided(s, start)
        b1 = base1[s, here, :]
        b2 = base2[s, here, :]
        r = sigma * inverse
        q = b2 * inverse
        pairs = [
            (b2, sigma), (b1, r), (b2, r), (b1, q), (b2, q), (r, r), (r, q), (q, q),
            (b1, b2), (b2, b2), (b1, sigma), (b2, sig1[s, here, :]),
        ]
        return tuple(t + fold(x * y) for t, (x, y) in zip(totals, pairs))

    sum_start(2, lax.fori_loop(0, blocks * steps, sums2, (zero,) * 12))
    more = sum_finish(2)
    theta2 = more(0)
    weight1 = more(1) - theta2 * more(3)
    weight2 = more(2) - theta2 * more(4)
    length2 = (
        (more(5) - 2.0 * theta2 * more(6) + theta2 * theta2 * more(7))
        - 2.0 * (weight1 * weight1 + weight2 * weight2)
        + weight1 * weight1 * first_gram
        + 2.0 * weight1 * weight2 * more(8)
        + weight2 * weight2 * more(9)
    )
    scale2 = 1.0 / jnp.sqrt(jnp.maximum(length2, 0.0) + epsilon)

    def corr2(s, start):
        here = pl.ds(start, step)
        b1 = base1[s, here, :]
        b2 = base2[s, here, :]
        corr = (sig2[s, here, :] - theta2 * b2) * divided(s, start)
        return (corr - weight1 * b1 - weight2 * b2) * scale2

    def cross(i, totals):
        s, start = chunk(i)
        here = pl.ds(start, step)
        b3 = last[s, here, :]
        pairs = [(b3, sig1[s, here, :]), (b3, sig2[s, here, :])]
        return tuple(t + fold(x * y) for t, (x, y) in zip(totals, pairs))

    crossed = spread(
        ext3, last, corr2, lambda: lax.fori_loop(0, blocks * steps, cross, (zero,) * 2)
    )

    def sums3(s, totals):
        acc[s] = product(ext3, s, True)

        def inner(k, totals):
            here = pl.ds(pl.multiple_of(k * step, step), step)
            sigma = acc[s, here, :]
            vectors = [ref[blocks + s, here, :].astype(F32) for ref in (ext1, ext2, ext3)]
            return tuple(t + fold(v * sigma) for t, v in zip(totals, vectors))

        return lax.fori_loop(0, width // step, inner, totals)

    sum_start(3, list(lax.fori_loop(0, blocks, sums3, (zero,) * 3)) + list(crossed))
    end = sum_finish(3)
    cells = [
        [theta1, more(10), end(0)],
        [more(11), theta2, end(1)],
        [end(3), end(4), end(2)],
    ]
    row = lax.broadcasted_iota(jnp.int32, (8, 128), 0)
    col = lax.broadcasted_iota(jnp.int32, (8, 128), 1)
    out = zero
    for i in range(3):
        for j in range(3):
            out = jnp.where((row == i) & (col == j), cells[i][j], out)
    proj[...] = out


def on_device(psi, left, right, connect, sector_dims, precond):
    blocks, width = psi.shape[0], psi.shape[1]
    terms = left.shape[0]
    pieces, devices = lax.axis_size("term"), lax.axis_size("sector")
    count = pieces * devices
    share = width // pieces
    entries = float(blocks * devices * width * width)
    sizes = (pieces, devices, terms, blocks, width, entries)
    others = max(pieces - 1, 1)
    dma = pltpu.SemaphoreType.DMA
    vmem = pl.BlockSpec(memory_space=pltpu.VMEM)
    smem = pl.BlockSpec(memory_space=pltpu.SMEM)
    proj, last, env = pl.pallas_call(
        functools.partial(kernel, sizes),
        name="davidson",
        out_shape=(
            jax.ShapeDtypeStruct((8, 128), F32),
            jax.ShapeDtypeStruct((blocks, share, width), F32),
            jax.ShapeDtypeStruct((terms, blocks, width, width), BF16),
        ),
        in_specs=[smem, smem, vmem, vmem, vmem, vmem],
        out_specs=(vmem, vmem, vmem),
        scratch_shapes=[
            pltpu.VMEM((3 * blocks, width, width), BF16),
            pltpu.VMEM((3 * blocks, width, width), BF16),
            pltpu.VMEM((3 * blocks, width, width), BF16),
            pltpu.VMEM((3 * blocks, width, width), BF16),
            pltpu.VMEM((blocks, width, width), F32),
            pltpu.VMEM((others, blocks, share, width), BF16),
            pltpu.VMEM((others, blocks, share, width), BF16),
            pltpu.VMEM((blocks, share, width), F32),
            pltpu.VMEM((blocks, share, width), F32),
            pltpu.VMEM((blocks, share, width), F32),
            pltpu.VMEM((blocks, share, width), F32),
            pltpu.VMEM((4, ROWS, 128), F32),
            pltpu.VMEM((4, count, ROWS, 128), F32),
            dma((2, pieces, blocks)),
            dma((2, pieces, blocks)),
            dma((others, blocks)),
            dma((others, blocks)),
            dma((others, blocks)),
            dma((others, blocks)),
            dma((4,)),
            dma((4,)),
        ],
        compiler_params=pltpu.CompilerParams(
            collective_id=0, has_side_effects=True, vmem_limit_bytes=60 * 1024 * 1024
        ),
    )(sector_dims, connect, psi, left, right, precond)
    return proj[:3, :3], last, env


def solution(mesh):
    placed = (
        P("sector", None, None),
        P("term", "sector", None, None),
        P("term", "sector", None, None),
        P("term", "sector"),
        P(None, "sector"),
        P("sector", None, None),
    )
    return jax.shard_map(
        on_device,
        mesh=mesh,
        in_specs=placed,
        out_specs=(P(), P("sector", "term", None), P("term", "sector", None, None)),
        check_vma=False,
    )
```

```python
import functools
import jax
import jax.numpy as jnp
from jax import lax
from jax.experimental import pallas as pl
from jax.experimental.pallas import tpu as pltpu
from jax.sharding import PartitionSpec as P

epsilon = 1e-06
MESH = pl.DeviceIdType.MESH
F32 = jnp.float32
BF16 = jnp.bfloat16


def fold(values):
    rows, width = values.shape
    total = values.reshape(rows // 8, 8, width).sum(axis=0)
    out = total[:, :128]
    for start in range(128, width, 128):
        out = out + total[:, start : start + 128]
    return out


def kernel(
    sizes,
    dims, conn, psi, left_in, right_in, pre_in,
    proj, last, env_out,
    left, right, pre, env, raw, ext1, ext2, ext3, acc, stage, came, sig1, sig2, base1, base2, tile, slots,
    halo_send, halo_recv, relay_send, share_send, share_recv, part_send, part_recv, sum_send, sum_recv, load, store,
):
    pieces, devices, terms, blocks, width, entries = sizes
    share = width // pieces
    count = pieces * devices
    step = min(32, share)
    steps = share // step
    me_t = lax.axis_index("term")
    me_s = lax.axis_index("sector")
    me = me_t * devices + me_s
    first = me_s * blocks - blocks
    has_low = me_s > 0
    has_high = me_s < devices - 1
    odd = lax.rem(me_s, 2) == 1
    even = jnp.logical_not(odd)
    zero = jnp.zeros((8, 128), F32)

    def device_at(offset):
        other = lax.rem(me + offset, count)
        return (other // devices, lax.rem(other, devices))

    def term_at(offset):
        return lax.rem(me_t + offset, pieces)

    def rows_of(piece):
        return pl.ds(pl.multiple_of(piece * share, share), share)

    half = blocks // 2
    loads = [
        pltpu.make_async_copy(source, target, load.at[i])
        for i, (source, target) in enumerate(
            ((left_in, left), (right_in, right), (pre_in, pre))
        )
    ]
    for one in loads:
        one.start()
    barrier = pltpu.get_barrier_semaphore()

    @pl.loop(1, count)
    def _(offset):
        pl.semaphore_signal(barrier, inc=1, device_id=device_at(offset), device_id_type=MESH)

    pl.semaphore_wait(barrier, count - 1)

    def halo_copy(ref, s, j, up, rows):
        slot = s if up else 2 * blocks + s
        direction = 0 if up else 1
        return pltpu.make_async_remote_copy(
            src_ref=ref.at[blocks + s, rows],
            dst_ref=ref.at[slot, rows],
            send_sem=halo_send.at[direction, j, s],
            recv_sem=halo_recv.at[direction, j, s],
            device_id=(me_t, me_s + 1 if up else me_s - 1),
            device_id_type=MESH,
        )

    def sends(j, s, relayed):
        if j == 0:
            return has_high, has_low
        far = s < relayed
        return (
            has_high & jnp.logical_not(odd & far),
            has_low & jnp.logical_not(even & far),
        )

    def halo_start(ref, s, j, relayed):
        rows = rows_of(term_at(pieces - j))
        up, down = sends(j, s, relayed)

        @pl.when(up)
        def _():
            halo_copy(ref, s, j, True, rows).start()

        @pl.when(down)
        def _():
            halo_copy(ref, s, j, False, rows).start()

    def relay_copy(ref, s, j, up):
        slot = s if up else 2 * blocks + s
        return pltpu.make_async_remote_copy(
            src_ref=ref.at[slot, rows_of(me_t)],
            dst_ref=ref.at[slot, rows_of(me_t)],
            send_sem=relay_send.at[j - 1, s],
            recv_sem=halo_recv.at[0 if up else 1, j, s],
            device_id=(term_at(j), me_s),
            device_id_type=MESH,
        )

    def relay(ref, s, relayed):
        for up, here in ((True, has_low & even), (False, has_high & odd)):

            @pl.when(here & (s < relayed))
            def _():
                halo_copy(ref, s, 0, up, rows_of(me_t)).wait_recv()
                for j in range(1, pieces):
                    relay_copy(ref, s, j, up).start()

    def halo_wait(ref, s, relayed):
        far = s < relayed
        for j in range(pieces):
            rows = rows_of(term_at(pieces - j))
            up, down = sends(j, s, relayed)

            @pl.when(up)
            def _():
                halo_copy(ref, s, j, True, rows).wait_send()

            @pl.when(down)
            def _():
                halo_copy(ref, s, j, False, rows).wait_send()

            low, high = has_low, has_high
            if j == 0:
                low = low & jnp.logical_not(even & far)
                high = high & jnp.logical_not(odd & far)

            @pl.when(low)
            def _():
                halo_copy(ref, s, j, True, rows).wait_recv()

            @pl.when(high)
            def _():
                halo_copy(ref, s, j, False, rows).wait_recv()

        for up, here in ((True, has_low & even), (False, has_high & odd)):

            @pl.when(here & far)
            def _():
                for j in range(1, pieces):
                    relay_copy(ref, s, j, up).wait_send()

    def share_copy(ref, s, offset, piece):
        return pltpu.make_async_remote_copy(
            src_ref=ref.at[blocks + s, rows_of(piece)],
            dst_ref=ref.at[blocks + s, rows_of(piece)],
            send_sem=share_send.at[offset - 1, s],
            recv_sem=share_recv.at[offset - 1, s],
            device_id=(term_at(offset), me_s),
            device_id_type=MESH,
        )

    def part_copy(s, offset):
        return pltpu.make_async_remote_copy(
            src_ref=stage.at[offset - 1, s],
            dst_ref=came.at[offset - 1, s],
            send_sem=part_send.at[offset - 1, s],
            recv_sem=part_recv.at[offset - 1, s],
            device_id=(term_at(offset), me_s),
            device_id_type=MESH,
        )

    lane = lax.broadcasted_iota(jnp.int32, (1, 128), 1)

    def sum_start(which, tiles):
        packed = jnp.zeros((1, 128), F32)
        for i, one in enumerate(tiles):
            row = jnp.sum(one, axis=0, keepdims=True)
            packed = jnp.where(lane == i, jnp.sum(row, axis=1, keepdims=True), packed)
        tile[which] = packed
        slots[which, me] = packed

        @pl.loop(1, count)
        def _(offset):
            pltpu.make_async_remote_copy(
                src_ref=tile.at[which],
                dst_ref=slots.at[which, me],
                send_sem=sum_send.at[which],
                recv_sem=sum_recv.at[which],
                device_id=device_at(offset),
                device_id_type=MESH,
            ).start()

    def sum_finish(which):
        others = slots.at[which, pl.ds(0, count - 1)]
        pltpu.make_async_copy(others, others, sum_recv.at[which]).wait()
        pltpu.make_async_copy(others, others, sum_send.at[which]).wait()
        full = jnp.sum(slots[which], axis=0) / entries
        return lambda i: full[:, i : i + 1]

    row_ids = lax.broadcasted_iota(jnp.int32, (width, width), 0)
    col_ids = lax.broadcasted_iota(jnp.int32, (width, width), 1)

    @pl.loop(0, blocks)
    def _(s):
        keep = (row_ids < dims[0, s]) & (col_ids < dims[1, s])
        raw[blocks + s] = jnp.where(keep, psi[s].astype(F32), 0.0).astype(BF16)
        for j in range(pieces):
            halo_start(raw, s, j, blocks)

    def chunk(i):
        return i // steps, pl.multiple_of(lax.rem(i, steps) * step, step)

    def own_rows(start):
        return pl.ds(pl.multiple_of(me_t * share + start, step), step)

    def norm_step(i, total):
        s, start = chunk(i)
        v = raw[blocks + s, own_rows(start), :].astype(F32)
        return total + fold(v * v)

    sum_start(0, [lax.fori_loop(0, blocks * steps, norm_step, zero)])
    @pl.loop(0, blocks)
    def _(s):
        relay(raw, s, blocks)

    norm = sum_finish(0)(0)
    scale = 1.0 / jnp.sqrt(norm + epsilon)

    def scaled(slot):
        ext1[slot] = (raw[slot].astype(F32) * scale).astype(BF16)

    @pl.loop(0, blocks)
    def _(s):
        scaled(blocks + s)
        base1[s] = raw[blocks + s, rows_of(me_t), :].astype(F32) * scale

    @pl.loop(0, blocks)
    def _(s):
        halo_wait(raw, s, blocks)

        @pl.when(has_low)
        def _():
            scaled(s)

        @pl.when(has_high)
        def _():
            scaled(2 * blocks + s)

    def product(ref, s, keep):
        halves = []
        for t in range(terms):
            source = ref[jnp.clip(conn[t, s] - first, 0, 3 * blocks - 1)]
            one = jnp.dot(left[t, s], source, preferred_element_type=F32).astype(BF16)
            halves.append(one)
            if keep:
                env[t, s] = one
        total = None
        for t in range(terms):
            one = lax.dot_general(
                halves[t], right[t, s], (((1,), (1,)), ((), ())), preferred_element_type=F32
            )
            total = one if total is None else total + one
        return total

    def apply(ref):
        @pl.loop(0, blocks)
        def _(s):
            acc[s] = product(ref, s, False)
            for offset in range(1, pieces):
                stage[offset - 1, s] = acc[s, rows_of(term_at(offset)), :].astype(BF16)
                part_copy(s, offset).start()

    def masked_sum(s, start):
        total = acc[s, own_rows(start), :]
        for offset in range(1, pieces):
            total = total + came[offset - 1, s, pl.ds(start, step), :].astype(F32)
        rows = lax.broadcasted_iota(jnp.int32, (step, width), 0) + (me_t * share + start)
        cols = lax.broadcasted_iota(jnp.int32, (step, width), 1)
        return jnp.where((rows < dims[0, s]) & (cols < dims[1, s]), total, 0.0)

    def divided(s, start):
        return 1.0 / pre[s, own_rows(start), :].astype(F32)

    def part_wait(s):
        for offset in range(1, pieces):
            part_copy(s, offset).wait()

    def spread(ref, out, corr_of, meanwhile=None):
        @pl.loop(0, blocks)
        def _(s):
            @pl.loop(0, steps)
            def _(k):
                start = pl.multiple_of(k * step, step)
                value = corr_of(s, start)
                out[s, pl.ds(start, step), :] = value
                ref[blocks + s, own_rows(start), :] = value.astype(BF16)

            for offset in range(1, pieces):
                share_copy(ref, s, offset, me_t).start()
            halo_start(ref, s, 0, half)

        @pl.loop(0, blocks)
        def _(s):
            for offset in range(1, pieces):
                share_copy(ref, s, offset, term_at(pieces - offset)).wait_recv()
                halo_start(ref, s, offset, half)
            relay(ref, s, half)

        extra = meanwhile() if meanwhile is not None else None

        @pl.loop(0, blocks)
        def _(s):
            for offset in range(1, pieces):
                share_copy(ref, s, offset, me_t).wait_send()
            halo_wait(ref, s, half)
        return extra

    for one in loads:
        one.wait()
    apply(ext1)

    def sums1(i, totals):
        s, start = chunk(i)
        here = pl.ds(start, step)

        @pl.when(start == 0)
        def _():
            part_wait(s)

        sigma = masked_sum(s, start)
        sig1[s, here, :] = sigma
        inverse = divided(s, start)
        b1 = base1[s, here, :]
        r = sigma * inverse
        q = b1 * inverse
        pairs = [(b1, sigma), (b1, r), (b1, q), (r, r), (r, q), (q, q), (b1, b1)]
        return tuple(t + fold(x * y) for t, (x, y) in zip(totals, pairs))

    sum_start(1, lax.fori_loop(0, blocks * steps, sums1, (zero,) * 7))
    got = sum_finish(1)
    theta1 = got(0)
    first_gram = got(6)
    weight = got(1) - theta1 * got(2)
    length = (
        (got(3) - 2.0 * theta1 * got(4) + theta1 * theta1 * got(5))
        - 2.0 * weight * weight
        + weight * weight * first_gram
    )
    scale1 = 1.0 / jnp.sqrt(jnp.maximum(length, 0.0) + epsilon)

    def corr1(s, start):
        here = pl.ds(start, step)
        b1 = base1[s, here, :]
        corr = (sig1[s, here, :] - theta1 * b1) * divided(s, start)
        return (corr - weight * b1) * scale1

    spread(ext2, base2, corr1)

    apply(ext2)

    def sums2(i, totals):
        s, start = chunk(i)
        here = pl.ds(start, step)

        @pl.when(start == 0)
        def _():
            part_wait(s)

        sigma = masked_sum(s, start)
        sig2[s, here, :] = sigma
        inverse = divided(s, start)
        b1 = base1[s, here, :]
        b2 = base2[s, here, :]
        r = sigma * inverse
        q = b2 * inverse
        pairs = [
            (b2, sigma), (b1, r), (b2, r), (b1, q), (b2, q), (r, r), (r, q), (q, q),
            (b1, b2), (b2, b2), (b1, sigma), (b2, sig1[s, here, :]),
        ]
        return tuple(t + fold(x * y) for t, (x, y) in zip(totals, pairs))

    sum_start(2, lax.fori_loop(0, blocks * steps, sums2, (zero,) * 12))
    more = sum_finish(2)
    theta2 = more(0)
    weight1 = more(1) - theta2 * more(3)
    weight2 = more(2) - theta2 * more(4)
    length2 = (
        (more(5) - 2.0 * theta2 * more(6) + theta2 * theta2 * more(7))
        - 2.0 * (weight1 * weight1 + weight2 * weight2)
        + weight1 * weight1 * first_gram
        + 2.0 * weight1 * weight2 * more(8)
        + weight2 * weight2 * more(9)
    )
    scale2 = 1.0 / jnp.sqrt(jnp.maximum(length2, 0.0) + epsilon)

    def corr2(s, start):
        here = pl.ds(start, step)
        b1 = base1[s, here, :]
        b2 = base2[s, here, :]
        corr = (sig2[s, here, :] - theta2 * b2) * divided(s, start)
        return (corr - weight1 * b1 - weight2 * b2) * scale2

    def cross(i, totals):
        s, start = chunk(i)
        here = pl.ds(start, step)
        b3 = last[s, here, :]
        pairs = [(b3, sig1[s, here, :]), (b3, sig2[s, here, :])]
        return tuple(t + fold(x * y) for t, (x, y) in zip(totals, pairs))

    crossed = spread(
        ext3, last, corr2, lambda: lax.fori_loop(0, blocks * steps, cross, (zero,) * 2)
    )

    def sums3(s, totals):
        acc[s] = product(ext3, s, True)

        def inner(k, totals):
            here = pl.ds(pl.multiple_of(k * step, step), step)
            sigma = acc[s, here, :]
            vectors = [ref[blocks + s, here, :].astype(F32) for ref in (ext1, ext2, ext3)]
            return tuple(t + fold(v * sigma) for t, v in zip(totals, vectors))

        return lax.fori_loop(0, width // step, inner, totals)

    sum_start(3, list(lax.fori_loop(0, blocks, sums3, (zero,) * 3)) + list(crossed))

    def env_copy(t, s):
        return pltpu.make_async_copy(env.at[t, s], env_out.at[t, s], store.at[t, s])

    @pl.loop(0, blocks)
    def _(s):
        own = ext3[blocks + s]
        for t in range(terms):
            new = lax.dot_general(
                own, env[t, s], (((0,), (0,)), ((), ())), preferred_element_type=F32
            )
            env[t, s] = (new * width ** (-0.5)).astype(BF16)
            env_copy(t, s).start()

    end = sum_finish(3)
    cells = [
        [theta1, more(10), end(0)],
        [more(11), theta2, end(1)],
        [end(3), end(4), end(2)],
    ]
    row = lax.broadcasted_iota(jnp.int32, (8, 128), 0)
    col = lax.broadcasted_iota(jnp.int32, (8, 128), 1)
    out = zero
    for i in range(3):
        for j in range(3):
            out = jnp.where((row == i) & (col == j), cells[i][j], out)
    proj[...] = out

    @pl.loop(0, blocks)
    def _(s):
        for t in range(terms):
            env_copy(t, s).wait()


def on_device(psi, left, right, connect, sector_dims, precond):
    blocks, width = psi.shape[0], psi.shape[1]
    terms = left.shape[0]
    pieces, devices = lax.axis_size("term"), lax.axis_size("sector")
    count = pieces * devices
    share = width // pieces
    entries = float(blocks * devices * width * width)
    sizes = (pieces, devices, terms, blocks, width, entries)
    others = max(pieces - 1, 1)
    dma = pltpu.SemaphoreType.DMA
    vmem = pl.BlockSpec(memory_space=pltpu.VMEM)
    smem = pl.BlockSpec(memory_space=pltpu.SMEM)
    anywhere = pl.BlockSpec(memory_space=pl.ANY)
    proj, last, env = pl.pallas_call(
        functools.partial(kernel, sizes),
        name="davidson",
        out_shape=(
            jax.ShapeDtypeStruct((8, 128), F32),
            jax.ShapeDtypeStruct((blocks, share, width), F32),
            jax.ShapeDtypeStruct((terms, blocks, width, width), BF16),
        ),
        in_specs=[smem, smem, vmem, anywhere, anywhere, anywhere],
        out_specs=(vmem, vmem, anywhere),
        scratch_shapes=[
            pltpu.VMEM((terms, blocks, width, width), BF16),
            pltpu.VMEM((terms, blocks, width, width), BF16),
            pltpu.VMEM((blocks, width, width), BF16),
            pltpu.VMEM((terms, blocks, width, width), BF16),
            pltpu.VMEM((3 * blocks, width, width), BF16),
            pltpu.VMEM((3 * blocks, width, width), BF16),
            pltpu.VMEM((3 * blocks, width, width), BF16),
            pltpu.VMEM((3 * blocks, width, width), BF16),
            pltpu.VMEM((blocks, width, width), F32),
            pltpu.VMEM((others, blocks, share, width), BF16),
            pltpu.VMEM((others, blocks, share, width), BF16),
            pltpu.VMEM((blocks, share, width), F32),
            pltpu.VMEM((blocks, share, width), F32),
            pltpu.VMEM((blocks, share, width), F32),
            pltpu.VMEM((blocks, share, width), F32),
            pltpu.VMEM((4, 1, 128), F32),
            pltpu.VMEM((4, count, 1, 128), F32),
            dma((2, pieces, blocks)),
            dma((2, pieces, blocks)),
            dma((others, blocks)),
            dma((others, blocks)),
            dma((others, blocks)),
            dma((others, blocks)),
            dma((others, blocks)),
            dma((4,)),
            dma((4,)),
            dma((3,)),
            dma((terms, blocks)),
        ],
        compiler_params=pltpu.CompilerParams(
            collective_id=0, has_side_effects=True, vmem_limit_bytes=60 * 1024 * 1024
        ),
    )(sector_dims, connect, psi, left, right, precond)
    return proj[:3, :3], last, env


def solution(mesh):
    placed = (
        P("sector", None, None),
        P("term", "sector", None, None),
        P("term", "sector", None, None),
        P("term", "sector"),
        P(None, "sector"),
        P("sector", None, None),
    )
    return jax.shard_map(
        on_device,
        mesh=mesh,
        in_specs=placed,
        out_specs=(P(), P("sector", "term", None), P("term", "sector", None, None)),
        check_vma=False,
    )
```

```python
import functools
import jax
import jax.numpy as jnp
from jax import lax
from jax.experimental import pallas as pl
from jax.experimental.pallas import tpu as pltpu
from jax.sharding import PartitionSpec as P

epsilon = 1e-06
MESH = pl.DeviceIdType.MESH
F32 = jnp.float32
BF16 = jnp.bfloat16


def fold(values):
    rows, width = values.shape
    total = values.reshape(rows // 8, 8, width).sum(axis=0)
    out = total[:, :128]
    for start in range(128, width, 128):
        out = out + total[:, start : start + 128]
    return out


def kernel(
    sizes,
    dims, conn, psi_in, left_in, right_in, pre_in,
    proj, last_out, env_out,
    left, right, pre, env, psi, last, inverse_of, raw, ext1, ext2, ext3, acc, stage, came, sig1, sig2, base1, base2, tile, slots,
    halo_send, halo_recv, relay_send, share_send, share_recv, part_send, part_recv, sum_send, sum_recv, load, store,
):
    pieces, devices, terms, blocks, width, entries = sizes
    share = width // pieces
    count = pieces * devices
    step = min(32, share)
    steps = share // step
    me_t = lax.axis_index("term")
    me_s = lax.axis_index("sector")
    me = me_t * devices + me_s
    first = me_s * blocks - blocks
    has_low = me_s > 0
    has_high = me_s < devices - 1
    odd = lax.rem(me_s, 2) == 1
    even = jnp.logical_not(odd)
    zero = jnp.zeros((8, 128), F32)

    def device_at(offset):
        other = lax.rem(me + offset, count)
        return (other // devices, lax.rem(other, devices))

    def term_at(offset):
        return lax.rem(me_t + offset, pieces)

    def rows_of(piece):
        return pl.ds(pl.multiple_of(piece * share, share), share)

    half = blocks // 2
    loads = [
        pltpu.make_async_copy(source, target, load.at[i])
        for i, (source, target) in enumerate(
            ((psi_in, psi), (pre_in, pre), (left_in, left), (right_in, right))
        )
    ]
    for one in loads:
        one.start()
    barrier = pltpu.get_barrier_semaphore()

    @pl.loop(1, count)
    def _(offset):
        pl.semaphore_signal(barrier, inc=1, device_id=device_at(offset), device_id_type=MESH)

    def halo_copy(ref, s, j, up, rows):
        slot = s if up else 2 * blocks + s
        direction = 0 if up else 1
        return pltpu.make_async_remote_copy(
            src_ref=ref.at[blocks + s, rows],
            dst_ref=ref.at[slot, rows],
            send_sem=halo_send.at[direction, j, s],
            recv_sem=halo_recv.at[direction, j, s],
            device_id=(me_t, me_s + 1 if up else me_s - 1),
            device_id_type=MESH,
        )

    def sends(j, s, relayed):
        if j == 0:
            return has_high, has_low
        far = s < relayed
        return (
            has_high & jnp.logical_not(odd & far),
            has_low & jnp.logical_not(even & far),
        )

    def halo_start(ref, s, j, relayed):
        rows = rows_of(term_at(pieces - j))
        up, down = sends(j, s, relayed)

        @pl.when(up)
        def _():
            halo_copy(ref, s, j, True, rows).start()

        @pl.when(down)
        def _():
            halo_copy(ref, s, j, False, rows).start()

    def relay_copy(ref, s, j, up):
        slot = s if up else 2 * blocks + s
        return pltpu.make_async_remote_copy(
            src_ref=ref.at[slot, rows_of(me_t)],
            dst_ref=ref.at[slot, rows_of(me_t)],
            send_sem=relay_send.at[j - 1, s],
            recv_sem=halo_recv.at[0 if up else 1, j, s],
            device_id=(term_at(j), me_s),
            device_id_type=MESH,
        )

    def relay(ref, s, relayed):
        for up, here in ((True, has_low & even), (False, has_high & odd)):

            @pl.when(here & (s < relayed))
            def _():
                halo_copy(ref, s, 0, up, rows_of(me_t)).wait_recv()
                for j in range(1, pieces):
                    relay_copy(ref, s, j, up).start()

    def halo_wait(ref, s, relayed):
        far = s < relayed
        for j in range(pieces):
            rows = rows_of(term_at(pieces - j))
            up, down = sends(j, s, relayed)

            @pl.when(up)
            def _():
                halo_copy(ref, s, j, True, rows).wait_send()

            @pl.when(down)
            def _():
                halo_copy(ref, s, j, False, rows).wait_send()

            low, high = has_low, has_high
            if j == 0:
                low = low & jnp.logical_not(even & far)
                high = high & jnp.logical_not(odd & far)

            @pl.when(low)
            def _():
                halo_copy(ref, s, j, True, rows).wait_recv()

            @pl.when(high)
            def _():
                halo_copy(ref, s, j, False, rows).wait_recv()

        for up, here in ((True, has_low & even), (False, has_high & odd)):

            @pl.when(here & far)
            def _():
                for j in range(1, pieces):
                    relay_copy(ref, s, j, up).wait_send()

    def share_copy(ref, s, offset, piece):
        return pltpu.make_async_remote_copy(
            src_ref=ref.at[blocks + s, rows_of(piece)],
            dst_ref=ref.at[blocks + s, rows_of(piece)],
            send_sem=share_send.at[offset - 1, s],
            recv_sem=share_recv.at[offset - 1, s],
            device_id=(term_at(offset), me_s),
            device_id_type=MESH,
        )

    def part_copy(s, offset):
        return pltpu.make_async_remote_copy(
            src_ref=stage.at[offset - 1, s],
            dst_ref=came.at[offset - 1, s],
            send_sem=part_send.at[offset - 1, s],
            recv_sem=part_recv.at[offset - 1, s],
            device_id=(term_at(offset), me_s),
            device_id_type=MESH,
        )

    lane = lax.broadcasted_iota(jnp.int32, (1, 128), 1)

    def sum_start(which, tiles):
        packed = jnp.zeros((1, 128), F32)
        for i, one in enumerate(tiles):
            row = jnp.sum(one, axis=0, keepdims=True)
            packed = jnp.where(lane == i, jnp.sum(row, axis=1, keepdims=True), packed)
        tile[which] = packed
        slots[which, me] = packed

        @pl.loop(1, count)
        def _(offset):
            pltpu.make_async_remote_copy(
                src_ref=tile.at[which],
                dst_ref=slots.at[which, me],
                send_sem=sum_send.at[which],
                recv_sem=sum_recv.at[which],
                device_id=device_at(offset),
                device_id_type=MESH,
            ).start()

    def sum_finish(which):
        others = slots.at[which, pl.ds(0, count - 1)]
        pltpu.make_async_copy(others, others, sum_recv.at[which]).wait()
        pltpu.make_async_copy(others, others, sum_send.at[which]).wait()
        full = jnp.sum(slots[which], axis=0) / entries
        return lambda i: full[:, i : i + 1]

    row_ids = lax.broadcasted_iota(jnp.int32, (width, width), 0)
    col_ids = lax.broadcasted_iota(jnp.int32, (width, width), 1)

    loads[0].wait()

    @pl.loop(0, blocks)
    def _(s):
        keep = (row_ids < dims[0, s]) & (col_ids < dims[1, s])
        raw[blocks + s] = jnp.where(keep, psi[s].astype(F32), 0.0).astype(BF16)

    pl.semaphore_wait(barrier, count - 1)

    @pl.loop(0, blocks)
    def _(s):
        for j in range(pieces):
            halo_start(raw, s, j, blocks)

    starts = [k * step for k in range(steps)]

    def own_rows(start):
        return pl.ds(pl.multiple_of(me_t * share + start, step), step)

    def norm_step(s, total):
        for start in starts:
            v = raw[blocks + s, own_rows(start), :].astype(F32)
            total = total + fold(v * v)
        return total

    sum_start(0, [lax.fori_loop(0, blocks, norm_step, zero)])
    loads[1].wait()

    @pl.loop(0, blocks)
    def _(s):
        for start in starts:
            inverse_of[s, pl.ds(start, step), :] = 1.0 / pre[s, own_rows(start), :].astype(F32)

    @pl.loop(0, blocks)
    def _(s):
        relay(raw, s, blocks)

    norm = sum_finish(0)(0)
    scale = 1.0 / jnp.sqrt(norm + epsilon)

    def scaled(slot):
        ext1[slot] = (raw[slot].astype(F32) * scale).astype(BF16)

    @pl.loop(0, blocks)
    def _(s):
        scaled(blocks + s)
        base1[s] = raw[blocks + s, rows_of(me_t), :].astype(F32) * scale

    @pl.loop(0, blocks)
    def _(s):
        halo_wait(raw, s, blocks)

        @pl.when(has_low)
        def _():
            scaled(s)

        @pl.when(has_high)
        def _():
            scaled(2 * blocks + s)

    def product(ref, s, keep):
        halves = []
        for t in range(terms):
            source = ref[jnp.clip(conn[t, s] - first, 0, 3 * blocks - 1)]
            one = jnp.dot(left[t, s], source, preferred_element_type=F32).astype(BF16)
            halves.append(one)
            if keep:
                env[t, s] = one
        total = None
        for t in range(terms):
            one = lax.dot_general(
                halves[t], right[t, s], (((1,), (1,)), ((), ())), preferred_element_type=F32
            )
            total = one if total is None else total + one
        return total

    def apply(ref):
        @pl.loop(0, blocks)
        def _(s):
            acc[s] = product(ref, s, False)
            for offset in range(1, pieces):
                stage[offset - 1, s] = acc[s, rows_of(term_at(offset)), :].astype(BF16)
                part_copy(s, offset).start()

    def masked_sum(s, start):
        total = acc[s, own_rows(start), :]
        for offset in range(1, pieces):
            total = total + came[offset - 1, s, pl.ds(start, step), :].astype(F32)
        rows = lax.broadcasted_iota(jnp.int32, (step, width), 0) + (me_t * share + start)
        cols = lax.broadcasted_iota(jnp.int32, (step, width), 1)
        return jnp.where((rows < dims[0, s]) & (cols < dims[1, s]), total, 0.0)

    def divided(s, start):
        return inverse_of[s, pl.ds(start, step), :]

    def part_wait(s):
        for offset in range(1, pieces):
            part_copy(s, offset).wait()

    def spread(ref, out, corr_of, meanwhile=None):
        @pl.loop(0, blocks)
        def _(s):
            for start in starts:
                value = corr_of(s, start)
                out[s, pl.ds(start, step), :] = value
                ref[blocks + s, own_rows(start), :] = value.astype(BF16)

            for offset in range(1, pieces):
                share_copy(ref, s, offset, me_t).start()
            halo_start(ref, s, 0, half)

        @pl.loop(0, blocks)
        def _(s):
            for offset in range(1, pieces):
                share_copy(ref, s, offset, term_at(pieces - offset)).wait_recv()
                halo_start(ref, s, offset, half)
            relay(ref, s, half)

        extra = meanwhile() if meanwhile is not None else None

        @pl.loop(0, blocks)
        def _(s):
            for offset in range(1, pieces):
                share_copy(ref, s, offset, me_t).wait_send()
            halo_wait(ref, s, half)
        return extra

    loads[2].wait()
    loads[3].wait()
    apply(ext1)

    def sums1(s, totals):
        part_wait(s)
        for start in starts:
            totals = sums1_rows(s, start, totals)
        return totals

    def sums1_rows(s, start, totals):
        here = pl.ds(start, step)
        sigma = masked_sum(s, start)
        sig1[s, here, :] = sigma
        inverse = divided(s, start)
        b1 = base1[s, here, :]
        r = sigma * inverse
        q = b1 * inverse
        pairs = [(b1, sigma), (b1, r), (b1, q), (r, r), (r, q), (q, q), (b1, b1)]
        return tuple(t + fold(x * y) for t, (x, y) in zip(totals, pairs))

    sum_start(1, lax.fori_loop(0, blocks, sums1, (zero,) * 7))
    got = sum_finish(1)
    theta1 = got(0)
    first_gram = got(6)
    weight = got(1) - theta1 * got(2)
    length = (
        (got(3) - 2.0 * theta1 * got(4) + theta1 * theta1 * got(5))
        - 2.0 * weight * weight
        + weight * weight * first_gram
    )
    scale1 = 1.0 / jnp.sqrt(jnp.maximum(length, 0.0) + epsilon)

    def corr1(s, start):
        here = pl.ds(start, step)
        b1 = base1[s, here, :]
        corr = (sig1[s, here, :] - theta1 * b1) * divided(s, start)
        return (corr - weight * b1) * scale1

    spread(ext2, base2, corr1)

    apply(ext2)

    def sums2(s, totals):
        part_wait(s)
        for start in starts:
            totals = sums2_rows(s, start, totals)
        return totals

    def sums2_rows(s, start, totals):
        here = pl.ds(start, step)
        sigma = masked_sum(s, start)
        sig2[s, here, :] = sigma
        inverse = divided(s, start)
        b1 = base1[s, here, :]
        b2 = base2[s, here, :]
        r = sigma * inverse
        q = b2 * inverse
        pairs = [
            (b2, sigma), (b1, r), (b2, r), (b1, q), (b2, q), (r, r), (r, q), (q, q),
            (b1, b2), (b2, b2), (b1, sigma), (b2, sig1[s, here, :]),
        ]
        return tuple(t + fold(x * y) for t, (x, y) in zip(totals, pairs))

    sum_start(2, lax.fori_loop(0, blocks, sums2, (zero,) * 12))
    more = sum_finish(2)
    theta2 = more(0)
    weight1 = more(1) - theta2 * more(3)
    weight2 = more(2) - theta2 * more(4)
    length2 = (
        (more(5) - 2.0 * theta2 * more(6) + theta2 * theta2 * more(7))
        - 2.0 * (weight1 * weight1 + weight2 * weight2)
        + weight1 * weight1 * first_gram
        + 2.0 * weight1 * weight2 * more(8)
        + weight2 * weight2 * more(9)
    )
    scale2 = 1.0 / jnp.sqrt(jnp.maximum(length2, 0.0) + epsilon)

    def corr2(s, start):
        here = pl.ds(start, step)
        b1 = base1[s, here, :]
        b2 = base2[s, here, :]
        corr = (sig2[s, here, :] - theta2 * b2) * divided(s, start)
        return (corr - weight1 * b1 - weight2 * b2) * scale2

    def cross(s, totals):
        for start in starts:
            here = pl.ds(start, step)
            b3 = last[s, here, :]
            pairs = [(b3, sig1[s, here, :]), (b3, sig2[s, here, :])]
            totals = tuple(t + fold(x * y) for t, (x, y) in zip(totals, pairs))
        return totals

    last_copy = pltpu.make_async_copy(last, last_out, load.at[0])

    def meanwhile():
        last_copy.start()
        return lax.fori_loop(0, blocks, cross, (zero,) * 2)

    crossed = spread(ext3, last, corr2, meanwhile)

    def sums3(s, totals):
        acc[s] = product(ext3, s, True)

        for start in range(0, width, step):
            here = pl.ds(start, step)
            sigma = acc[s, here, :]
            vectors = [ref[blocks + s, here, :].astype(F32) for ref in (ext1, ext2, ext3)]
            totals = tuple(t + fold(v * sigma) for t, v in zip(totals, vectors))
        return totals

    sum_start(3, list(lax.fori_loop(0, blocks, sums3, (zero,) * 3)) + list(crossed))

    def env_copy(t, s):
        return pltpu.make_async_copy(env.at[t, s], env_out.at[t, s], store.at[t, s])

    @pl.loop(0, blocks)
    def _(s):
        own = ext3[blocks + s]
        for t in range(terms):
            new = lax.dot_general(
                own, env[t, s], (((0,), (0,)), ((), ())), preferred_element_type=F32
            )
            env[t, s] = (new * width ** (-0.5)).astype(BF16)
            env_copy(t, s).start()

    end = sum_finish(3)
    cells = [
        [theta1, more(10), end(0)],
        [more(11), theta2, end(1)],
        [end(3), end(4), end(2)],
    ]
    row = lax.broadcasted_iota(jnp.int32, (8, 128), 0)
    col = lax.broadcasted_iota(jnp.int32, (8, 128), 1)
    out = zero
    for i in range(3):
        for j in range(3):
            out = jnp.where((row == i) & (col == j), cells[i][j], out)
    proj[...] = out

    @pl.loop(0, blocks)
    def _(s):
        for t in range(terms):
            env_copy(t, s).wait()

    last_copy.wait()


def on_device(psi, left, right, connect, sector_dims, precond):
    blocks, width = psi.shape[0], psi.shape[1]
    terms = left.shape[0]
    pieces, devices = lax.axis_size("term"), lax.axis_size("sector")
    count = pieces * devices
    share = width // pieces
    entries = float(blocks * devices * width * width)
    sizes = (pieces, devices, terms, blocks, width, entries)
    others = max(pieces - 1, 1)
    dma = pltpu.SemaphoreType.DMA
    vmem = pl.BlockSpec(memory_space=pltpu.VMEM)
    smem = pl.BlockSpec(memory_space=pltpu.SMEM)
    anywhere = pl.BlockSpec(memory_space=pl.ANY)
    proj, last, env = pl.pallas_call(
        functools.partial(kernel, sizes),
        name="davidson",
        out_shape=(
            jax.ShapeDtypeStruct((8, 128), F32),
            jax.ShapeDtypeStruct((blocks, share, width), F32),
            jax.ShapeDtypeStruct((terms, blocks, width, width), BF16),
        ),
        in_specs=[smem, smem, anywhere, anywhere, anywhere, anywhere],
        out_specs=(vmem, anywhere, anywhere),
        scratch_shapes=[
            pltpu.VMEM((terms, blocks, width, width), BF16),
            pltpu.VMEM((terms, blocks, width, width), BF16),
            pltpu.VMEM((blocks, width, width), BF16),
            pltpu.VMEM((terms, blocks, width, width), BF16),
            pltpu.VMEM((blocks, width, width), BF16),
            pltpu.VMEM((blocks, share, width), F32),
            pltpu.VMEM((blocks, share, width), F32),
            pltpu.VMEM((3 * blocks, width, width), BF16),
            pltpu.VMEM((3 * blocks, width, width), BF16),
            pltpu.VMEM((3 * blocks, width, width), BF16),
            pltpu.VMEM((3 * blocks, width, width), BF16),
            pltpu.VMEM((blocks, width, width), F32),
            pltpu.VMEM((others, blocks, share, width), BF16),
            pltpu.VMEM((others, blocks, share, width), BF16),
            pltpu.VMEM((blocks, share, width), F32),
            pltpu.VMEM((blocks, share, width), F32),
            pltpu.VMEM((blocks, share, width), F32),
            pltpu.VMEM((blocks, share, width), F32),
            pltpu.VMEM((4, 1, 128), F32),
            pltpu.VMEM((4, count, 1, 128), F32),
            dma((2, pieces, blocks)),
            dma((2, pieces, blocks)),
            dma((others, blocks)),
            dma((others, blocks)),
            dma((others, blocks)),
            dma((others, blocks)),
            dma((others, blocks)),
            dma((4,)),
            dma((4,)),
            dma((4,)),
            dma((terms, blocks)),
        ],
        compiler_params=pltpu.CompilerParams(
            collective_id=0, has_side_effects=True, vmem_limit_bytes=60 * 1024 * 1024
        ),
    )(sector_dims, connect, psi, left, right, precond)
    return proj[:3, :3], last, env


def solution(mesh):
    placed = (
        P("sector", None, None),
        P("term", "sector", None, None),
        P("term", "sector", None, None),
        P("term", "sector"),
        P(None, "sector"),
        P("sector", None, None),
    )
    return jax.shard_map(
        on_device,
        mesh=mesh,
        in_specs=placed,
        out_specs=(P(), P("sector", "term", None), P("term", "sector", None, None)),
        check_vma=False,
    )
```

```python
import functools
import jax
import jax.numpy as jnp
from jax import lax
from jax.experimental import pallas as pl
from jax.experimental.pallas import tpu as pltpu
from jax.sharding import PartitionSpec as P

epsilon = 1e-06
MESH = pl.DeviceIdType.MESH
F32 = jnp.float32
BF16 = jnp.bfloat16


def fold(values):
    rows, width = values.shape
    total = values.reshape(rows // 8, 8, width).sum(axis=0)
    out = total[:, :128]
    for start in range(128, width, 128):
        out = out + total[:, start : start + 128]
    return out


def kernel(
    sizes,
    dims, conn, psi_in, left_in, right_in, pre_in,
    proj, last_out, env_out,
    left, right, pre, env, psi, last, inverse_of, raw, ext1, ext2, ext3, acc, stage, came, sig1, sig2, base1, base2, tile, slots,
    halo_send, halo_recv, relay_send, share_send, share_recv, part_send, part_recv, sum_send, sum_recv, load, store,
):
    pieces, devices, terms, blocks, width, entries = sizes
    share = width // pieces
    count = pieces * devices
    step = min(32, share)
    steps = share // step
    me_t = lax.axis_index("term")
    me_s = lax.axis_index("sector")
    me = me_t * devices + me_s
    first = me_s * blocks - blocks
    has_low = me_s > 0
    has_high = me_s < devices - 1
    odd = lax.rem(me_s, 2) == 1
    even = jnp.logical_not(odd)
    zero = jnp.zeros((8, 128), F32)

    def device_at(offset):
        other = lax.rem(me + offset, count)
        return (other // devices, lax.rem(other, devices))

    def term_at(offset):
        return lax.rem(me_t + offset, pieces)

    def rows_of(piece):
        return pl.ds(pl.multiple_of(piece * share, share), share)

    half = blocks // 2
    loads = [
        pltpu.make_async_copy(source, target, load.at[i])
        for i, (source, target) in enumerate(
            ((psi_in, psi), (pre_in, pre), (left_in, left), (right_in, right))
        )
    ]
    for one in loads:
        one.start()
    barrier = pltpu.get_barrier_semaphore()

    @pl.loop(1, count)
    def _(offset):
        pl.semaphore_signal(barrier, inc=1, device_id=device_at(offset), device_id_type=MESH)

    def halo_copy(ref, s, j, up, rows):
        slot = s if up else 2 * blocks + s
        direction = 0 if up else 1
        return pltpu.make_async_remote_copy(
            src_ref=ref.at[blocks + s, rows],
            dst_ref=ref.at[slot, rows],
            send_sem=halo_send.at[direction, j, s],
            recv_sem=halo_recv.at[direction, j, s],
            device_id=(me_t, me_s + 1 if up else me_s - 1),
            device_id_type=MESH,
        )

    def sends(j, s, relayed):
        if j == 0:
            return has_high, has_low
        far = s < relayed
        return (
            has_high & jnp.logical_not(odd & far),
            has_low & jnp.logical_not(even & far),
        )

    def halo_start(ref, s, j, relayed):
        rows = rows_of(term_at(pieces - j))
        up, down = sends(j, s, relayed)

        @pl.when(up)
        def _():
            halo_copy(ref, s, j, True, rows).start()

        @pl.when(down)
        def _():
            halo_copy(ref, s, j, False, rows).start()

    def relay_copy(ref, s, j, up):
        slot = s if up else 2 * blocks + s
        return pltpu.make_async_remote_copy(
            src_ref=ref.at[slot, rows_of(me_t)],
            dst_ref=ref.at[slot, rows_of(me_t)],
            send_sem=relay_send.at[j - 1, s],
            recv_sem=halo_recv.at[0 if up else 1, j, s],
            device_id=(term_at(j), me_s),
            device_id_type=MESH,
        )

    def relay(ref, s, relayed):
        for up, here in ((True, has_low & even), (False, has_high & odd)):

            @pl.when(here & (s < relayed))
            def _():
                halo_copy(ref, s, 0, up, rows_of(me_t)).wait_recv()
                for j in range(1, pieces):
                    relay_copy(ref, s, j, up).start()

    def halo_wait(ref, s, relayed):
        far = s < relayed
        for j in range(pieces):
            rows = rows_of(term_at(pieces - j))
            up, down = sends(j, s, relayed)

            @pl.when(up)
            def _():
                halo_copy(ref, s, j, True, rows).wait_send()

            @pl.when(down)
            def _():
                halo_copy(ref, s, j, False, rows).wait_send()

            low, high = has_low, has_high
            if j == 0:
                low = low & jnp.logical_not(even & far)
                high = high & jnp.logical_not(odd & far)

            @pl.when(low)
            def _():
                halo_copy(ref, s, j, True, rows).wait_recv()

            @pl.when(high)
            def _():
                halo_copy(ref, s, j, False, rows).wait_recv()

        for up, here in ((True, has_low & even), (False, has_high & odd)):

            @pl.when(here & far)
            def _():
                for j in range(1, pieces):
                    relay_copy(ref, s, j, up).wait_send()

    def share_copy(ref, s, offset, piece):
        return pltpu.make_async_remote_copy(
            src_ref=ref.at[blocks + s, rows_of(piece)],
            dst_ref=ref.at[blocks + s, rows_of(piece)],
            send_sem=share_send.at[offset - 1, s],
            recv_sem=share_recv.at[offset - 1, s],
            device_id=(term_at(offset), me_s),
            device_id_type=MESH,
        )

    def part_copy(s, offset):
        return pltpu.make_async_remote_copy(
            src_ref=stage.at[offset - 1, s],
            dst_ref=came.at[offset - 1, s],
            send_sem=part_send.at[offset - 1, s],
            recv_sem=part_recv.at[offset - 1, s],
            device_id=(term_at(offset), me_s),
            device_id_type=MESH,
        )

    lane = lax.broadcasted_iota(jnp.int32, (1, 128), 1)

    def sum_start(which, tiles):
        packed = jnp.zeros((1, 128), F32)
        for i, one in enumerate(tiles):
            row = jnp.sum(one, axis=0, keepdims=True)
            packed = jnp.where(lane == i, jnp.sum(row, axis=1, keepdims=True), packed)
        tile[which] = packed
        slots[which, me] = packed

        @pl.loop(1, count)
        def _(offset):
            pltpu.make_async_remote_copy(
                src_ref=tile.at[which],
                dst_ref=slots.at[which, me],
                send_sem=sum_send.at[which],
                recv_sem=sum_recv.at[which],
                device_id=device_at(offset),
                device_id_type=MESH,
            ).start()

    def sum_finish(which):
        others = slots.at[which, pl.ds(0, count - 1)]
        pltpu.make_async_copy(others, others, sum_recv.at[which]).wait()
        full = jnp.sum(slots[which], axis=0) / entries
        return lambda i: full[:, i : i + 1]

    row_ids = lax.broadcasted_iota(jnp.int32, (width, width), 0)
    col_ids = lax.broadcasted_iota(jnp.int32, (width, width), 1)

    loads[0].wait()

    @pl.loop(0, blocks)
    def _(s):
        keep = (row_ids < dims[0, s]) & (col_ids < dims[1, s])
        raw[blocks + s] = jnp.where(keep, psi[s].astype(F32), 0.0).astype(BF16)

    pl.semaphore_wait(barrier, count - 1)

    @pl.loop(0, blocks)
    def _(s):
        for j in range(pieces):
            halo_start(raw, s, j, blocks)

    starts = [k * step for k in range(steps)]

    def own_rows(start):
        return pl.ds(pl.multiple_of(me_t * share + start, step), step)

    def norm_step(s, total):
        for start in starts:
            v = raw[blocks + s, own_rows(start), :].astype(F32)
            total = total + fold(v * v)
        return total

    sum_start(0, [lax.fori_loop(0, blocks, norm_step, zero)])
    loads[1].wait()

    @pl.loop(0, blocks)
    def _(s):
        for start in starts:
            inverse_of[s, pl.ds(start, step), :] = 1.0 / pre[s, own_rows(start), :].astype(F32)

    @pl.loop(0, blocks)
    def _(s):
        relay(raw, s, blocks)

    norm = sum_finish(0)(0)
    scale = 1.0 / jnp.sqrt(norm + epsilon)

    def scaled(slot):
        ext1[slot] = (raw[slot].astype(F32) * scale).astype(BF16)

    @pl.loop(0, blocks)
    def _(s):
        scaled(blocks + s)
        base1[s] = raw[blocks + s, rows_of(me_t), :].astype(F32) * scale

    @pl.loop(0, blocks)
    def _(s):
        halo_wait(raw, s, blocks)

        @pl.when(has_low)
        def _():
            scaled(s)

        @pl.when(has_high)
        def _():
            scaled(2 * blocks + s)

    def product(ref, s, keep):
        halves = []
        for t in range(terms):
            source = ref[jnp.clip(conn[t, s] - first, 0, 3 * blocks - 1)]
            one = jnp.dot(left[t, s], source, preferred_element_type=F32).astype(BF16)
            halves.append(one)
            if keep:
                env[t, s] = one
        total = None
        for t in range(terms):
            one = lax.dot_general(
                halves[t], right[t, s], (((1,), (1,)), ((), ())), preferred_element_type=F32
            )
            total = one if total is None else total + one
        return total

    def apply(ref):
        @pl.loop(0, blocks)
        def _(s):
            acc[s] = product(ref, s, False)
            for offset in range(1, pieces):
                stage[offset - 1, s] = acc[s, rows_of(term_at(offset)), :].astype(BF16)
                part_copy(s, offset).start()

    def masked_sum(s, start):
        total = acc[s, own_rows(start), :]
        for offset in range(1, pieces):
            total = total + came[offset - 1, s, pl.ds(start, step), :].astype(F32)
        rows = lax.broadcasted_iota(jnp.int32, (step, width), 0) + (me_t * share + start)
        cols = lax.broadcasted_iota(jnp.int32, (step, width), 1)
        return jnp.where((rows < dims[0, s]) & (cols < dims[1, s]), total, 0.0)

    def divided(s, start):
        return inverse_of[s, pl.ds(start, step), :]

    def part_wait(s):
        for offset in range(1, pieces):
            part_copy(s, offset).wait()

    def spread(ref, out, corr_of, meanwhile=None):
        @pl.loop(0, blocks)
        def _(s):
            for start in starts:
                value = corr_of(s, start)
                out[s, pl.ds(start, step), :] = value
                ref[blocks + s, own_rows(start), :] = value.astype(BF16)

            for offset in range(1, pieces):
                share_copy(ref, s, offset, me_t).start()
            halo_start(ref, s, 0, half)

        @pl.loop(0, blocks)
        def _(s):
            for offset in range(1, pieces):
                share_copy(ref, s, offset, term_at(pieces - offset)).wait_recv()
                halo_start(ref, s, offset, half)
            relay(ref, s, half)

        extra = meanwhile() if meanwhile is not None else None

        @pl.loop(0, blocks)
        def _(s):
            for offset in range(1, pieces):
                share_copy(ref, s, offset, me_t).wait_send()
            halo_wait(ref, s, half)
        return extra

    loads[2].wait()
    loads[3].wait()
    apply(ext1)

    def sums1(s, totals):
        part_wait(s)
        for start in starts:
            totals = sums1_rows(s, start, totals)
        return totals

    def sums1_rows(s, start, totals):
        here = pl.ds(start, step)
        sigma = masked_sum(s, start)
        sig1[s, here, :] = sigma
        inverse = divided(s, start)
        b1 = base1[s, here, :]
        r = sigma * inverse
        q = b1 * inverse
        pairs = [(b1, sigma), (b1, r), (b1, q), (r, r), (r, q), (q, q), (b1, b1)]
        return tuple(t + fold(x * y) for t, (x, y) in zip(totals, pairs))

    sum_start(1, lax.fori_loop(0, blocks, sums1, (zero,) * 7))
    got = sum_finish(1)
    theta1 = got(0)
    first_gram = got(6)
    weight = got(1) - theta1 * got(2)
    length = (
        (got(3) - 2.0 * theta1 * got(4) + theta1 * theta1 * got(5))
        - 2.0 * weight * weight
        + weight * weight * first_gram
    )
    scale1 = 1.0 / jnp.sqrt(jnp.maximum(length, 0.0) + epsilon)

    def corr1(s, start):
        here = pl.ds(start, step)
        b1 = base1[s, here, :]
        corr = (sig1[s, here, :] - theta1 * b1) * divided(s, start)
        return (corr - weight * b1) * scale1

    spread(ext2, base2, corr1)

    apply(ext2)

    def sums2(s, totals):
        part_wait(s)
        for start in starts:
            totals = sums2_rows(s, start, totals)
        return totals

    def sums2_rows(s, start, totals):
        here = pl.ds(start, step)
        sigma = masked_sum(s, start)
        sig2[s, here, :] = sigma
        inverse = divided(s, start)
        b1 = base1[s, here, :]
        b2 = base2[s, here, :]
        r = sigma * inverse
        q = b2 * inverse
        pairs = [
            (b2, sigma), (b1, r), (b2, r), (b1, q), (b2, q), (r, r), (r, q), (q, q),
            (b1, b2), (b2, b2), (b1, sigma), (b2, sig1[s, here, :]),
        ]
        return tuple(t + fold(x * y) for t, (x, y) in zip(totals, pairs))

    sum_start(2, lax.fori_loop(0, blocks, sums2, (zero,) * 12))
    more = sum_finish(2)
    theta2 = more(0)
    weight1 = more(1) - theta2 * more(3)
    weight2 = more(2) - theta2 * more(4)
    length2 = (
        (more(5) - 2.0 * theta2 * more(6) + theta2 * theta2 * more(7))
        - 2.0 * (weight1 * weight1 + weight2 * weight2)
        + weight1 * weight1 * first_gram
        + 2.0 * weight1 * weight2 * more(8)
        + weight2 * weight2 * more(9)
    )
    scale2 = 1.0 / jnp.sqrt(jnp.maximum(length2, 0.0) + epsilon)

    def corr2(s, start):
        here = pl.ds(start, step)
        b1 = base1[s, here, :]
        b2 = base2[s, here, :]
        corr = (sig2[s, here, :] - theta2 * b2) * divided(s, start)
        return (corr - weight1 * b1 - weight2 * b2) * scale2

    def cross(s, totals):
        for start in starts:
            here = pl.ds(start, step)
            b3 = last[s, here, :]
            pairs = [(b3, sig1[s, here, :]), (b3, sig2[s, here, :])]
            totals = tuple(t + fold(x * y) for t, (x, y) in zip(totals, pairs))
        return totals

    last_copy = pltpu.make_async_copy(last, last_out, load.at[0])

    def meanwhile():
        last_copy.start()
        return lax.fori_loop(0, blocks, cross, (zero,) * 2)

    crossed = spread(ext3, last, corr2, meanwhile)

    def sums3(s, totals):
        acc[s] = product(ext3, s, True)

        for start in range(0, width, step):
            here = pl.ds(start, step)
            sigma = acc[s, here, :]
            vectors = [ref[blocks + s, here, :].astype(F32) for ref in (ext1, ext2, ext3)]
            totals = tuple(t + fold(v * sigma) for t, v in zip(totals, vectors))
        return totals

    sum_start(3, list(lax.fori_loop(0, blocks, sums3, (zero,) * 3)) + list(crossed))

    def env_copy(t, s):
        return pltpu.make_async_copy(env.at[t, s], env_out.at[t, s], store.at[t, s])

    @pl.loop(0, blocks)
    def _(s):
        own = ext3[blocks + s]
        for t in range(terms):
            new = lax.dot_general(
                own, env[t, s], (((0,), (0,)), ((), ())), preferred_element_type=F32
            )
            env[t, s] = (new * width ** (-0.5)).astype(BF16)
            env_copy(t, s).start()

    end = sum_finish(3)
    cells = [
        [theta1, more(10), end(0)],
        [more(11), theta2, end(1)],
        [end(3), end(4), end(2)],
    ]
    row = lax.broadcasted_iota(jnp.int32, (8, 128), 0)
    col = lax.broadcasted_iota(jnp.int32, (8, 128), 1)
    out = zero
    for i in range(3):
        for j in range(3):
            out = jnp.where((row == i) & (col == j), cells[i][j], out)
    proj[...] = out

    @pl.loop(0, blocks)
    def _(s):
        for t in range(terms):
            env_copy(t, s).wait()

    last_copy.wait()
    for which in range(4):
        others = slots.at[which, pl.ds(0, count - 1)]
        pltpu.make_async_copy(others, others, sum_send.at[which]).wait()


def on_device(psi, left, right, connect, sector_dims, precond):
    blocks, width = psi.shape[0], psi.shape[1]
    terms = left.shape[0]
    pieces, devices = lax.axis_size("term"), lax.axis_size("sector")
    count = pieces * devices
    share = width // pieces
    entries = float(blocks * devices * width * width)
    sizes = (pieces, devices, terms, blocks, width, entries)
    others = max(pieces - 1, 1)
    dma = pltpu.SemaphoreType.DMA
    vmem = pl.BlockSpec(memory_space=pltpu.VMEM)
    smem = pl.BlockSpec(memory_space=pltpu.SMEM)
    anywhere = pl.BlockSpec(memory_space=pl.ANY)
    proj, last, env = pl.pallas_call(
        functools.partial(kernel, sizes),
        name="davidson",
        out_shape=(
            jax.ShapeDtypeStruct((8, 128), F32),
            jax.ShapeDtypeStruct((blocks, share, width), F32),
            jax.ShapeDtypeStruct((terms, blocks, width, width), BF16),
        ),
        in_specs=[smem, smem, anywhere, anywhere, anywhere, anywhere],
        out_specs=(vmem, anywhere, anywhere),
        scratch_shapes=[
            pltpu.VMEM((terms, blocks, width, width), BF16),
            pltpu.VMEM((terms, blocks, width, width), BF16),
            pltpu.VMEM((blocks, width, width), BF16),
            pltpu.VMEM((terms, blocks, width, width), BF16),
            pltpu.VMEM((blocks, width, width), BF16),
            pltpu.VMEM((blocks, share, width), F32),
            pltpu.VMEM((blocks, share, width), F32),
            pltpu.VMEM((3 * blocks, width, width), BF16),
            pltpu.VMEM((3 * blocks, width, width), BF16),
            pltpu.VMEM((3 * blocks, width, width), BF16),
            pltpu.VMEM((3 * blocks, width, width), BF16),
            pltpu.VMEM((blocks, width, width), F32),
            pltpu.VMEM((others, blocks, share, width), BF16),
            pltpu.VMEM((others, blocks, share, width), BF16),
            pltpu.VMEM((blocks, share, width), F32),
            pltpu.VMEM((blocks, share, width), F32),
            pltpu.VMEM((blocks, share, width), F32),
            pltpu.VMEM((blocks, share, width), F32),
            pltpu.VMEM((4, 1, 128), F32),
            pltpu.VMEM((4, count, 1, 128), F32),
            dma((2, pieces, blocks)),
            dma((2, pieces, blocks)),
            dma((others, blocks)),
            dma((others, blocks)),
            dma((others, blocks)),
            dma((others, blocks)),
            dma((others, blocks)),
            dma((4,)),
            dma((4,)),
            dma((4,)),
            dma((terms, blocks)),
        ],
        compiler_params=pltpu.CompilerParams(
            collective_id=0, has_side_effects=True, vmem_limit_bytes=60 * 1024 * 1024
        ),
    )(sector_dims, connect, psi, left, right, precond)
    return proj[:3, :3], last, env


def solution(mesh):
    placed = (
        P("sector", None, None),
        P("term", "sector", None, None),
        P("term", "sector", None, None),
        P("term", "sector"),
        P(None, "sector"),
        P("sector", None, None),
    )
    return jax.shard_map(
        on_device,
        mesh=mesh,
        in_specs=placed,
        out_specs=(P(), P("sector", "term", None), P("term", "sector", None, None)),
        check_vma=False,
    )
```
